32 devices in a mesh: parts: 2 (over y), wide: 4 (over z), rep: 2 (over x), sub: 2 (over core).
Axes of the slice: x: 2, y: 2, z: 4, core: 2. Of those that a mesh axis runs over, the one named last changes fastest.
Arguments:
- activations: bfloat16 [8, 2048, 512], P(('parts', 'wide'), 'sub'), parts along dimension 0, may hold values from -6 to 6
- deltas: bfloat16 [8, 2048, 512], P(('parts', 'wide'), 'sub'), parts along dimension 0, may hold values from -6 to 6
- act_factor: bfloat16 [512, 512], P(None, 'rep'), as said below
- delta_factor: bfloat16 [512, 512], P(None, 'rep'), as said below
- queries: bfloat16 [1280, 512, 512], P(None, ('rep', 'wide'), 'sub'), may hold values from -0.00059890747 to 0.00059890747
- assignment: int32 [8], P('parts'), parts along dimension 0, may hold values from 0 to 3, each once
- padding: int32 [8], P(('parts', 'wide')), parts along dimension 0, may hold values from 0 to 1023
Outputs:
- scores: float32 [8, 1280], P(('parts', 'wide'), ('rep', 'sub')), parts along dimension 0
The draws below stay inside these ranges and needn't reach their ends.
There are 2 independent parts, one for each index of `parts`. The reference program is written for one: setup_inputs(seed, part) draws one part's arguments, and reference() takes and returns one part's arrays. A program takes and returns all parts, laid end to end along the dimension named above; an argument that names none is the same for every part. Nothing has to cross between parts.
Inputs may be any that keep to these rules, and one draw needn't show every extreme that they name: `act_factor`: symmetric and positive definite. `delta_factor`: symmetric and positive definite. `assignment`: each number once.
All inputs are finite; a program needn't handle non-finite values.
Results may differ from the reference program's by a relative error of at most 0.005.
Values may be sent and summed in bfloat16 or wider, within the bound.
A program may use at most 128 MiB of HBM per device.

```python
import jax
import jax.numpy as jnp
from jax import lax

PROJ = 512
SEQ_LEN = 2048
QUERIES = 1280
SEQS = 4


def make_factor(key):
    first, second = jax.random.split(key)
    diag_part = jnp.exp(jax.random.uniform(first, (PROJ,), jnp.float32, jnp.log(0.5), jnp.log(2.0)))
    noise = jax.random.normal(second, (PROJ, PROJ), jnp.float32)
    symmetric = (noise + noise.T) * (0.2 / (2.0 * PROJ) ** 0.5)
    return (jnp.diag(diag_part) + symmetric).astype(jnp.bfloat16)


def draw_act_factor(key, part):
    return make_factor(jax.random.fold_in(key, 11))


def draw_delta_factor(key, part):
    return make_factor(jax.random.fold_in(key, 23))


def set_ends(values, rng, smallest, high):
    index_at = [jax.random.randint(jax.random.fold_in(rng, axis), (), 0, length) for axis, length in enumerate(values.shape)]
    longest = values.shape.index(max(values.shape))
    next_to = index_at[:longest] + [(index_at[longest] + 1) % values.shape[longest]] + index_at[longest + 1:]
    return values.at[tuple(index_at)].set(smallest).at[tuple(next_to)].set(high)


def with_spikes(entries, key, source, target, parts, factor):
    def block_of(dim):
        return (jnp.arange(entries.shape[dim]) // (entries.shape[dim] // parts)).reshape((-1,) + (1,) * (entries.ndim - 1 - dim))

    one_side = jax.random.permutation(key, parts)[block_of(target)]
    other_side = (block_of(target) + parts // 2) % parts
    return jnp.where((block_of(source) == one_side) | (block_of(source) == other_side), factor * entries, entries)


def level_of(stream_key, extent, shards, smallest, high):
    factor_of = 1.0
    for axis_at, shards_of in shards:
        draws = jax.random.uniform(jax.random.fold_in(jax.random.fold_in(stream_key, 6), axis_at), (shards_of,), jnp.float32, smallest / len(shards), high / len(shards))
        factor_of = factor_of * jnp.repeat(jnp.exp(draws), extent[axis_at] // shards_of).reshape((-1,) + (1,) * (len(extent) - 1 - axis_at))
    return factor_of


def scatter_about(key, extent, deviation, most, cuts=(), kind=jnp.bfloat16):
    result = deviation * jax.random.normal(key, extent, jnp.float32)
    if cuts:
        result = result * level_of(key, extent, cuts, -0.22, 0.18)
    return jnp.clip(result, -most, most).astype(kind)


def heavy_noise(rng, extent, deviation, reach, shards, heavy, dtype=jnp.bfloat16):
    drawn = deviation * jax.random.normal(rng, extent, jnp.float32)
    if shards:
        drawn = drawn * level_of(rng, extent, shards, -0.22, 0.18)
    return jnp.clip(with_spikes(drawn, jax.random.fold_in(rng, 3), *heavy), -reach, reach).astype(dtype)


def setup_inputs(seed: int = 0, part: int = 0) -> dict:
    seeds = jax.random.split(jax.random.key(seed), 8)
    own_keys = jax.random.split(jax.random.fold_in(seeds[7], part), 8)
    return {
        "activations": scatter_about(own_keys[0], (SEQS, SEQ_LEN, PROJ), 1.0, 6.0, ((0, 4), (1, 2))),
        "deltas": scatter_about(own_keys[1], (SEQS, SEQ_LEN, PROJ), 1.0, 6.0, ((0, 4), (1, 2))),
        "act_factor": draw_act_factor(jax.random.fold_in(seeds[7], 71), part),
        "delta_factor": draw_delta_factor(jax.random.fold_in(seeds[7], 71), part),
        "queries": heavy_noise(seeds[4], (QUERIES, PROJ, PROJ), 0.0001, 0.00059890747, ((1, 8), (2, 2)), (1, 0, 8, 2.0)),
        "assignment": jax.random.permutation(own_keys[5], SEQS).astype(jnp.int32),
        "padding": set_ends(jax.random.randint(own_keys[6], (SEQS,), 0, SEQ_LEN // 2), jax.random.fold_in(own_keys[6], 1), 0, (SEQ_LEN // 2) - 1).astype(jnp.int32),
    }


def reference(activations, deltas, act_factor, delta_factor, queries, assignment, padding):
    positions = lax.broadcasted_iota(jnp.int32, (SEQS, SEQ_LEN), 1)
    kept_mask = positions < (SEQ_LEN - padding)[:, None]
    masked = jnp.where(kept_mask[:, :, None], deltas, jnp.zeros((), jnp.bfloat16))
    delta_proj = jnp.dot(masked.reshape(SEQS * SEQ_LEN, PROJ), delta_factor, preferred_element_type=jnp.float32)
    delta_proj = delta_proj.astype(jnp.bfloat16).reshape(SEQS, SEQ_LEN, PROJ)
    act_proj = jnp.dot(activations.reshape(SEQS * SEQ_LEN, PROJ), act_factor, preferred_element_type=jnp.float32)
    act_proj = act_proj.astype(jnp.bfloat16).reshape(SEQS, SEQ_LEN, PROJ)
    grad = jnp.einsum("nti,ntj->nij", delta_proj.astype(jnp.float32), act_proj.astype(jnp.float32))
    grad = grad.astype(jnp.bfloat16)
    raw = jnp.dot(grad.reshape(SEQS, PROJ * PROJ), queries.reshape(QUERIES, PROJ * PROJ).T, preferred_element_type=jnp.float32)
    scores = jnp.zeros((SEQS, QUERIES), jnp.float32).at[assignment].set(raw)
    return scores
```

```python
import functools

import jax
import jax.numpy as jnp
from jax import lax
from jax.experimental import pallas as pl
from jax.experimental.pallas import tpu as pltpu
from jax.sharding import PartitionSpec as P

MESH = pl.DeviceIdType.MESH
GROUP = 32


def general_shards(
    activations, deltas, act_factor, delta_factor, queries, assignment, padding
):
    seq_dev, tok_dev, feature_width = activations.shape
    full_length = tok_dev * lax.axis_size("sub")
    token_start = lax.axis_index("sub") * tok_dev
    positions = token_start + lax.broadcasted_iota(jnp.int32, (seq_dev, tok_dev), 1)
    kept_mask = positions < (full_length - padding)[:, None]
    masked = jnp.where(kept_mask[:, :, None], deltas, jnp.zeros((), jnp.bfloat16))
    delta_proj = jnp.einsum(
        "stw,wi->sti", masked, delta_factor, preferred_element_type=jnp.float32
    ).astype(jnp.bfloat16)
    act_proj = jnp.einsum(
        "stw,wj->stj",
        activations,
        lax.all_gather(act_factor, "rep", axis=1, tiled=True),
        preferred_element_type=jnp.float32,
    ).astype(jnp.bfloat16)
    partial_value = jnp.einsum(
        "sti,stj->sij", delta_proj, act_proj, preferred_element_type=jnp.float32
    )
    summed = lax.psum_scatter(partial_value, "sub", scatter_dimension=2, tiled=True).astype(
        jnp.bfloat16
    )
    regrouped = lax.all_to_all(summed, "wide", split_axis=1, concat_axis=0, tiled=True)
    seq_total = regrouped.shape[0]
    grad_rows = regrouped.reshape(seq_total, -1)
    query_rows = queries.reshape(queries.shape[0], -1)
    partial_scores = lax.dot_general(
        grad_rows, query_rows, (((1,), (1,)), ((), ())), preferred_element_type=jnp.float32
    )
    inverse_order = (
        jnp.zeros((seq_total,), jnp.int32)
        .at[assignment]
        .set(jnp.arange(seq_total, dtype=jnp.int32))
    )
    ranked = jnp.take(partial_scores, inverse_order, axis=0)
    by_column = lax.psum_scatter(ranked, ("rep", "sub"), scatter_dimension=1, tiled=True)
    return lax.psum_scatter(by_column, "wide", scatter_dimension=0, tiled=True)


def kernel(
    n_wide,
    rows,
    assignment_ref,
    padding_ref,
    act_hbm,
    delta_hbm,
    act_factor_hbm,
    delta_factor_hbm,
    query_hbm,
    out_ref,
    act,
    delta,
    act_factor,
    delta_factor,
    query,
    diag,
    inner_mine,
    inner_theirs,
    factor_cols,
    grad,
    grad_all,
    weights,
    folded,
    outgoing,
    incoming,
    load_sem,
    query_sem,
    diag_sem,
    inner_sem,
    grad_send_sem,
    grad_recv_sem,
    score_send_sem,
    score_recv_sem,
):
    z = lax.axis_index("wide")
    r = lax.axis_index("rep")
    c = lax.axis_index("sub")
    n_rep, n_sub = 2, 2

    def peer(dz, dr, dc):
        return {
            "wide": lax.rem(z + dz, n_wide),
            "rep": lax.rem(r + dr, n_rep),
            "sub": lax.rem(c + dc, n_sub),
        }

    block_order = ((1, 1), (1, 0), (0, 1), (0, 0))
    everyone = [
        (dz, dr, dc) for dz in range(n_wide) for dr, dc in block_order if (dz, dr, dc) != (0, 0, 0)
    ]
    barrier = pltpu.get_barrier_semaphore()
    for offset in everyone:
        pl.semaphore_signal(barrier, inc=1, device_id=peer(*offset), device_id_type=MESH)

    loads = [
        pltpu.make_async_copy(src, dst, load_sem.at[k])
        for k, (src, dst) in enumerate(
            (
                (delta_factor_hbm, delta_factor),
                (delta_hbm, delta),
                (act_factor_hbm, act_factor),
                (act_hbm, act),
            )
        )
    ]
    for load in loads:
        load.start()

    chunk = GROUP * rows
    total = query.shape[0]
    block_groups = total // (chunk * n_rep * n_sub)

    def query_copy(place):
        span = pl.ds(pl.multiple_of(place * chunk, chunk), chunk)
        return pltpu.make_async_copy(query_hbm.at[span, :], query.at[span, :], query_sem.at[place])

    def block_at(dr, dc):
        return lax.rem(r + dr, n_rep) * n_sub + lax.rem(c + dc, n_sub)

    for dr, dc in block_order:
        first = block_at(dr, dc) * block_groups

        def begin(t, carry, first=first):
            query_copy(first + t).start()
            return carry

        lax.fori_loop(0, block_groups, begin, 0)

    loads[0].wait()
    loads[1].wait()
    tokens = delta.shape[0]
    half = act_factor.shape[1]
    limit = n_sub * tokens - padding_ref[0] - c * tokens
    position = lax.broadcasted_iota(jnp.int32, (tokens, half), 0)
    projected = jnp.dot(delta[...], delta_factor[...], preferred_element_type=jnp.float32)
    delta_proj = jnp.where(position < limit, projected, 0.0).astype(jnp.bfloat16)

    loads[2].wait()
    pl.semaphore_wait(barrier, len(everyone))
    diag_rows = pl.ds(pl.multiple_of(c * half, half), half)
    diag_copy = pltpu.make_async_remote_copy(
        src_ref=act_factor.at[diag_rows, :],
        dst_ref=diag,
        send_sem=diag_sem.at[0],
        recv_sem=diag_sem.at[1],
        device_id=peer(0, 1, 0),
        device_id_type=MESH,
    )

    @pl.when(r == c)
    def _():
        diag_copy.start()

    loads[3].wait()
    inner_mine[...] = lax.dot_general(
        delta_proj, act[...], (((0,), (0,)), ((), ())), preferred_element_type=jnp.float32
    )
    inner_copy = pltpu.make_async_remote_copy(
        src_ref=inner_mine,
        dst_ref=inner_theirs,
        send_sem=inner_sem.at[0],
        recv_sem=inner_sem.at[1],
        device_id=peer(0, 0, 1),
        device_id_type=MESH,
    )
    inner_copy.start()

    @pl.when(r == c)
    def _():
        factor_cols[...] = act_factor[...]
        diag_copy.wait_send()

    @pl.when(r != c)
    def _():
        mirrored = act_factor[diag_rows, :].astype(jnp.float32).T.astype(jnp.bfloat16)
        factor_cols[pl.ds(pl.multiple_of(r * half, half), half), :] = mirrored
        diag_copy.wait_recv()
        factor_cols[diag_rows, :] = diag[...]

    inner_copy.wait_recv()
    inner = inner_mine[...] + inner_theirs[...]
    high = inner.astype(jnp.bfloat16)
    low = (inner - high.astype(jnp.float32)).astype(jnp.bfloat16)
    gradient = jnp.dot(high, factor_cols[...], preferred_element_type=jnp.float32) + jnp.dot(
        low, factor_cols[...], preferred_element_type=jnp.float32
    )
    grad[...] = gradient.astype(jnp.bfloat16)
    mine = pl.ds(pl.multiple_of(z * rows, rows), rows)
    grad_copies = []
    for dz in range(n_wide - 1, 0, -1):
        target = pl.ds(pl.multiple_of(lax.rem(z + dz, n_wide) * rows, rows), rows)
        copy = pltpu.make_async_remote_copy(
            src_ref=grad.at[target, :],
            dst_ref=grad_all.at[mine, :],
            send_sem=grad_send_sem.at[dz],
            recv_sem=grad_recv_sem.at[dz],
            device_id=peer(dz, 0, 0),
            device_id_type=MESH,
        )
        copy.start()
        grad_copies.append(copy)
    grad_all[mine, :] = grad[mine, :]

    width = n_wide * rows
    lane = lax.broadcasted_iota(jnp.int32, (8, width), 1)
    sublane = lax.broadcasted_iota(jnp.int32, (8, width), 0)
    owner = lane // rows
    ranks = jnp.zeros((8, width), jnp.int32)
    for n in range(n_wide):
        ranks = jnp.where(owner == n, assignment_ref[n], ranks)
    places = jnp.where(ranks == sublane, 1.0, 0.0).astype(jnp.bfloat16)
    tile_of_lane = lax.rem(lane, rows) // 8
    on_diagonal = lax.rem(lane, 8) == sublane

    block_size = block_groups * GROUP
    folded[pl.ds(block_size, folded.shape[0] - block_size), :] = jnp.zeros(
        (folded.shape[0] - block_size, width), jnp.float32
    )
    inner_copy.wait_send()
    for copy in grad_copies:
        copy.wait_recv()
    weights[...] = grad_all[...].astype(jnp.float32).T.astype(jnp.bfloat16)

    score_copies = []
    for k, (dr, dc) in enumerate(block_order):
        first = block_at(dr, dc) * block_groups

        def step(t, carry, first=first):
            query_copy(first + t).wait()
            span = pl.ds(pl.multiple_of((first + t) * chunk, chunk), chunk)
            products = jnp.dot(
                query[span, :], weights[...], preferred_element_type=jnp.float32
            ).reshape(GROUP, rows // 8, 8, width)
            chosen = products[:, 0]
            for a in range(1, rows // 8):
                chosen = jnp.where((tile_of_lane == a)[None], products[:, a], chosen)
            chosen = jnp.where(on_diagonal[None], chosen, 0.0)
            folded[pl.ds(pl.multiple_of(t * GROUP, GROUP), GROUP), :] = jnp.sum(chosen, axis=1)
            return carry

        lax.fori_loop(0, block_groups, step, 0)
        sums = folded[...]
        sums_high = sums.astype(jnp.bfloat16)
        sums_low = (sums - sums_high.astype(jnp.float32)).astype(jnp.bfloat16)
        contract = (((1,), (1,)), ((), ()))
        ranked = lax.dot_general(
            places, sums_high, contract, preferred_element_type=jnp.float32
        ) + lax.dot_general(places, sums_low, contract, preferred_element_type=jnp.float32)
        for p in range(n_wide):
            outgoing[k, p] = ranked[p : p + 1, :]
        for dz in range(n_wide - 1, -1, -1):
            slot = k * n_wide + dz
            source = outgoing.at[k, lax.rem(z + dz, n_wide)]
            if (dz, dr, dc) == (0, 0, 0):
                continue
            copy = pltpu.make_async_remote_copy(
                src_ref=source,
                dst_ref=incoming.at[slot],
                send_sem=score_send_sem.at[slot],
                recv_sem=score_recv_sem.at[slot],
                device_id=peer(dz, dr, dc),
                device_id_type=MESH,
            )
            copy.start()
            score_copies.append((slot, copy))

    result = outgoing[len(block_order) - 1, z]
    for copy in grad_copies:
        copy.wait_send()
    for slot, copy in score_copies:
        copy.wait_send()
        copy.wait_recv()
        result = result + incoming[slot]
    out_ref[...] = result[:, :block_size]


def fused_shards(
    n_wide, activations, deltas, act_factor, delta_factor, queries, assignment, padding
):
    _, tokens, features = activations.shape
    n_queries, rows, columns = queries.shape
    half = act_factor.shape[1]
    width = n_wide * rows
    groups = n_queries // GROUP
    block_size = n_queries // 4
    padded = -(-block_size // 128) * 128
    hbm = pl.BlockSpec(memory_space=pl.ANY)
    smem = pl.BlockSpec(memory_space=pltpu.SMEM)
    dma = pltpu.SemaphoreType.DMA
    bf16, f32 = jnp.bfloat16, jnp.float32
    return pl.pallas_call(
        functools.partial(kernel, n_wide, rows),
        out_shape=jax.ShapeDtypeStruct((1, block_size), f32),
        in_specs=[smem, smem] + [hbm] * 5,
        out_specs=pl.BlockSpec(memory_space=pltpu.VMEM),
        scratch_shapes=[
            pltpu.VMEM((tokens, features), bf16),
            pltpu.VMEM((tokens, features), bf16),
            pltpu.VMEM((features, half), bf16),
            pltpu.VMEM((features, half), bf16),
            pltpu.VMEM((n_queries * rows, columns), bf16),
            pltpu.VMEM((half, half), bf16),
            pltpu.VMEM((half, features), f32),
            pltpu.VMEM((half, features), f32),
            pltpu.VMEM((features, half), bf16),
            pltpu.VMEM((half, columns), bf16),
            pltpu.VMEM((width, columns), bf16),
            pltpu.VMEM((columns, width), bf16),
            pltpu.VMEM((padded, width), f32),
            pltpu.VMEM((4, n_wide, 1, padded), f32),
            pltpu.VMEM((4 * n_wide, 1, padded), f32),
            dma((4,)),
            dma((groups,)),
            dma((2,)),
            dma((2,)),
            dma((n_wide,)),
            dma((n_wide,)),
            dma((4 * n_wide,)),
            dma((4 * n_wide,)),
        ],
        compiler_params=pltpu.CompilerParams(
            collective_id=0, has_side_effects=True, vmem_limit_bytes=60 * 1024 * 1024
        ),
    )(
        assignment,
        padding,
        activations.reshape(tokens, features),
        deltas.reshape(tokens, features),
        act_factor,
        delta_factor,
        queries.reshape(n_queries * rows, columns),
    )


def solution(mesh):
    placed = (
        P(("parts", "wide"), "sub", None),
        P(("parts", "wide"), "sub", None),
        P(None, "rep"),
        P(None, "rep"),
        P(None, ("rep", "wide"), "sub"),
        P("parts"),
        P(("parts", "wide")),
    )
    n_wide, n_rep, n_sub = (mesh.shape[name] for name in ("wide", "rep", "sub"))

    def shards(activations, deltas, act_factor, delta_factor, queries, assignment, padding):
        seq_dev, tokens, features = activations.shape
        n_queries, rows, columns = queries.shape
        fits = (
            seq_dev == 1
            and (n_rep, n_sub) == (2, 2)
            and n_wide <= 8
            and rows % 16 == 0
            and (n_wide * rows) % 128 == 0
            and columns % 128 == 0
            and act_factor.shape[1] == columns == n_wide * rows
            and tokens % 16 == 0
            and n_queries % (4 * GROUP) == 0
            and n_queries * rows * columns * 2 <= 44 * 2**20
        )
        run = functools.partial(fused_shards, n_wide) if fits else general_shards
        return run(activations, deltas, act_factor, delta_factor, queries, assignment, padding)

    return jax.shard_map(
        shards,
        mesh=mesh,
        in_specs=placed,
        out_specs=P(("parts", "wide"), ("rep", "sub")),
        check_vma=False,
    )
```

```python
import functools

import jax
import jax.numpy as jnp
from jax import lax
from jax.experimental import pallas as pl
from jax.experimental.pallas import tpu as pltpu
from jax.sharding import PartitionSpec as P

MESH = pl.DeviceIdType.MESH
GROUP = 160


def general_shards(
    activations, deltas, act_factor, delta_factor, queries, assignment, padding
):
    seq_dev, tok_dev, feature_width = activations.shape
    full_length = tok_dev * lax.axis_size("sub")
    token_start = lax.axis_index("sub") * tok_dev
    positions = token_start + lax.broadcasted_iota(jnp.int32, (seq_dev, tok_dev), 1)
    kept_mask = positions < (full_length - padding)[:, None]
    masked = jnp.where(kept_mask[:, :, None], deltas, jnp.zeros((), jnp.bfloat16))
    delta_proj = jnp.einsum(
        "stw,wi->sti", masked, delta_factor, preferred_element_type=jnp.float32
    ).astype(jnp.bfloat16)
    act_proj = jnp.einsum(
        "stw,wj->stj",
        activations,
        lax.all_gather(act_factor, "rep", axis=1, tiled=True),
        preferred_element_type=jnp.float32,
    ).astype(jnp.bfloat16)
    partial_value = jnp.einsum(
        "sti,stj->sij", delta_proj, act_proj, preferred_element_type=jnp.float32
    )
    summed = lax.psum_scatter(partial_value, "sub", scatter_dimension=2, tiled=True).astype(
        jnp.bfloat16
    )
    regrouped = lax.all_to_all(summed, "wide", split_axis=1, concat_axis=0, tiled=True)
    seq_total = regrouped.shape[0]
    grad_rows = regrouped.reshape(seq_total, -1)
    query_rows = queries.reshape(queries.shape[0], -1)
    partial_scores = lax.dot_general(
        grad_rows, query_rows, (((1,), (1,)), ((), ())), preferred_element_type=jnp.float32
    )
    inverse_order = (
        jnp.zeros((seq_total,), jnp.int32)
        .at[assignment]
        .set(jnp.arange(seq_total, dtype=jnp.int32))
    )
    ranked = jnp.take(partial_scores, inverse_order, axis=0)
    by_column = lax.psum_scatter(ranked, ("rep", "sub"), scatter_dimension=1, tiled=True)
    return lax.psum_scatter(by_column, "wide", scatter_dimension=0, tiled=True)


def kernel(
    n_wide,
    rows,
    assignment_ref,
    padding_ref,
    act_hbm,
    delta_hbm,
    act_factor_hbm,
    delta_factor_hbm,
    query_hbm,
    out_ref,
    act,
    delta,
    act_factor,
    delta_factor,
    query,
    diag,
    inner_mine,
    inner_theirs,
    factor_cols,
    grad,
    grad_all,
    weights,
    folded,
    outgoing,
    incoming,
    load_sem,
    query_sem,
    diag_sem,
    inner_sem,
    grad_send_sem,
    grad_recv_sem,
    score_send_sem,
    score_recv_sem,
):
    z = lax.axis_index("wide")
    r = lax.axis_index("rep")
    c = lax.axis_index("sub")
    n_rep, n_sub = 2, 2

    def peer(dz, dr, dc):
        return {
            "wide": lax.rem(z + dz, n_wide),
            "rep": lax.rem(r + dr, n_rep),
            "sub": lax.rem(c + dc, n_sub),
        }

    block_order = ((1, 1), (1, 0), (0, 1), (0, 0))
    everyone = [(0, 0, 1), (0, 1, 0)] + [(dz, 0, 0) for dz in range(n_wide - 1, 0, -1)]
    barrier = pltpu.get_barrier_semaphore()
    for offset in everyone:
        pl.semaphore_signal(barrier, inc=1, device_id=peer(*offset), device_id_type=MESH)

    loads = [
        pltpu.make_async_copy(src, dst, load_sem.at[k])
        for k, (src, dst) in enumerate(
            (
                (delta_factor_hbm, delta_factor),
                (delta_hbm, delta),
                (act_factor_hbm, act_factor),
                (act_hbm, act),
            )
        )
    ]
    for load in loads:
        load.start()

    chunk = GROUP * rows
    total = query.shape[0]
    block_groups = total // (chunk * n_rep * n_sub)

    def query_copy(place):
        span = pl.ds(pl.multiple_of(place * chunk, chunk), chunk)
        return pltpu.make_async_copy(query_hbm.at[span, :], query.at[span, :], query_sem.at[place])

    def block_at(dr, dc):
        return lax.rem(r + dr, n_rep) * n_sub + lax.rem(c + dc, n_sub)

    for dr, dc in block_order:
        first = block_at(dr, dc) * block_groups

        def begin(t, carry, first=first):
            query_copy(first + t).start()
            return carry

        lax.fori_loop(0, block_groups, begin, 0)

    half = act_factor.shape[1]
    pl.semaphore_wait(barrier, len(everyone))
    diag_rows = pl.ds(pl.multiple_of(c * half, half), half)
    diag_copy = pltpu.make_async_remote_copy(
        src_ref=act_factor_hbm.at[diag_rows, :],
        dst_ref=diag,
        send_sem=diag_sem.at[0],
        recv_sem=diag_sem.at[1],
        device_id=peer(0, 1, 0),
        device_id_type=MESH,
    )

    @pl.when(r == c)
    def _():
        diag_copy.start()

    loads[0].wait()
    loads[1].wait()
    tokens = delta.shape[0]
    limit = n_sub * tokens - padding_ref[0] - c * tokens
    position = lax.broadcasted_iota(jnp.int32, (tokens, half), 0)
    projected = jnp.dot(delta[...], delta_factor[...], preferred_element_type=jnp.float32)
    delta_proj = jnp.where(position < limit, projected, 0.0).astype(jnp.bfloat16)

    loads[2].wait()
    loads[3].wait()
    inner_mine[...] = lax.dot_general(
        delta_proj, act[...], (((0,), (0,)), ((), ())), preferred_element_type=jnp.float32
    )
    inner_copy = pltpu.make_async_remote_copy(
        src_ref=inner_mine,
        dst_ref=inner_theirs,
        send_sem=inner_sem.at[0],
        recv_sem=inner_sem.at[1],
        device_id=peer(0, 0, 1),
        device_id_type=MESH,
    )
    inner_copy.start()

    @pl.when(r == c)
    def _():
        factor_cols[...] = act_factor[...]
        diag_copy.wait_send()

    @pl.when(r != c)
    def _():
        mirrored = act_factor[diag_rows, :].astype(jnp.float32).T.astype(jnp.bfloat16)
        factor_cols[pl.ds(pl.multiple_of(r * half, half), half), :] = mirrored
        diag_copy.wait_recv()
        factor_cols[diag_rows, :] = diag[...]

    inner_copy.wait_recv()
    inner = inner_mine[...] + inner_theirs[...]
    high = inner.astype(jnp.bfloat16)
    low = (inner - high.astype(jnp.float32)).astype(jnp.bfloat16)
    gradient = jnp.dot(high, factor_cols[...], preferred_element_type=jnp.float32) + jnp.dot(
        low, factor_cols[...], preferred_element_type=jnp.float32
    )
    grad[...] = gradient.astype(jnp.bfloat16)
    mine = pl.ds(pl.multiple_of(z * rows, rows), rows)
    grad_copies = []
    for dz in range(n_wide - 1, 0, -1):
        target = pl.ds(pl.multiple_of(lax.rem(z + dz, n_wide) * rows, rows), rows)
        copy = pltpu.make_async_remote_copy(
            src_ref=grad.at[target, :],
            dst_ref=grad_all.at[mine, :],
            send_sem=grad_send_sem.at[dz],
            recv_sem=grad_recv_sem.at[dz],
            device_id=peer(dz, 0, 0),
            device_id_type=MESH,
        )
        copy.start()
        grad_copies.append(copy)
    grad_all[mine, :] = grad[mine, :]

    width = n_wide * rows
    lane = lax.broadcasted_iota(jnp.int32, (8, width), 1)
    sublane = lax.broadcasted_iota(jnp.int32, (8, width), 0)
    owner = lane // rows
    ranks = jnp.zeros((8, width), jnp.int32)
    for n in range(n_wide):
        ranks = jnp.where(owner == n, assignment_ref[n], ranks)
    places = jnp.where(ranks == sublane, 1.0, 0.0).astype(jnp.bfloat16)
    tile_of_lane = lax.rem(lane, rows) // 8
    on_diagonal = lax.rem(lane, 8) == sublane

    block_size = block_groups * GROUP
    folded[pl.ds(block_size, folded.shape[0] - block_size), :] = jnp.zeros(
        (folded.shape[0] - block_size, width), jnp.float32
    )
    inner_copy.wait_send()
    for copy in grad_copies:
        copy.wait_recv()
    weights[...] = grad_all[...].astype(jnp.float32).T.astype(jnp.bfloat16)

    def score_copy(k, dz):
        slot = k * n_wide + dz
        return pltpu.make_async_remote_copy(
            src_ref=outgoing.at[k, lax.rem(z + dz, n_wide)],
            dst_ref=incoming.at[slot],
            send_sem=score_send_sem.at[slot],
            recv_sem=score_recv_sem.at[slot],
            device_id=peer(dz, 1 - k // n_sub, 1 - lax.rem(k, n_sub)),
            device_id_type=MESH,
        )

    last = len(block_order) - 1

    def score_block(k, carry):
        first = block_at(1 - k // n_sub, 1 - lax.rem(k, n_sub)) * block_groups

        def score_group(t, inner_carry):
            query_copy(first + t).wait()
            span = pl.ds(pl.multiple_of((first + t) * chunk, chunk), chunk)
            products = jnp.dot(
                query[span, :], weights[...], preferred_element_type=jnp.float32
            ).reshape(GROUP, rows // 8, 8, width)
            chosen = products[:, 0]
            for a in range(1, rows // 8):
                chosen = jnp.where((tile_of_lane == a)[None], products[:, a], chosen)
            chosen = jnp.where(on_diagonal[None], chosen, 0.0)
            folded[pl.ds(pl.multiple_of(t * GROUP, GROUP), GROUP), :] = jnp.sum(chosen, axis=1)
            return inner_carry

        lax.fori_loop(0, block_groups, score_group, 0)
        sums = folded[...]
        sums_high = sums.astype(jnp.bfloat16)
        sums_low = (sums - sums_high.astype(jnp.float32)).astype(jnp.bfloat16)
        contract = (((1,), (1,)), ((), ()))
        ranked = lax.dot_general(
            places, sums_high, contract, preferred_element_type=jnp.float32
        ) + lax.dot_general(places, sums_low, contract, preferred_element_type=jnp.float32)
        for p in range(n_wide):
            outgoing[k, p] = ranked[p : p + 1, :]
        for dz in range(n_wide - 1, 0, -1):
            score_copy(k, dz).start()

        @pl.when(k < last)
        def _():
            score_copy(k, 0).start()

        return carry

    lax.fori_loop(0, len(block_order), score_block, 0)

    result = outgoing[last, z]
    for copy in grad_copies:
        copy.wait_send()
    for k in range(last + 1):
        for dz in range(n_wide - 1, -1, -1):
            if (k, dz) != (last, 0):
                score_copy(k, dz).wait()
                result = result + incoming[k * n_wide + dz]
    out_ref[...] = result[:, :block_size]


def fused_shards(
    n_wide, activations, deltas, act_factor, delta_factor, queries, assignment, padding
):
    _, tokens, features = activations.shape
    n_queries, rows, columns = queries.shape
    half = act_factor.shape[1]
    width = n_wide * rows
    groups = n_queries // GROUP
    block_size = n_queries // 4
    padded = -(-block_size // 128) * 128
    hbm = pl.BlockSpec(memory_space=pl.ANY)
    smem = pl.BlockSpec(memory_space=pltpu.SMEM)
    dma = pltpu.SemaphoreType.DMA
    bf16, f32 = jnp.bfloat16, jnp.float32
    return pl.pallas_call(
        functools.partial(kernel, n_wide, rows),
        out_shape=jax.ShapeDtypeStruct((1, block_size), f32),
        in_specs=[smem, smem] + [hbm] * 5,
        out_specs=pl.BlockSpec(memory_space=pltpu.VMEM),
        scratch_shapes=[
            pltpu.VMEM((tokens, features), bf16),
            pltpu.VMEM((tokens, features), bf16),
            pltpu.VMEM((features, half), bf16),
            pltpu.VMEM((features, half), bf16),
            pltpu.VMEM((n_queries * rows, columns), bf16),
            pltpu.VMEM((half, half), bf16),
            pltpu.VMEM((half, features), f32),
            pltpu.VMEM((half, features), f32),
            pltpu.VMEM((features, half), bf16),
            pltpu.VMEM((half, columns), bf16),
            pltpu.VMEM((width, columns), bf16),
            pltpu.VMEM((columns, width), bf16),
            pltpu.VMEM((padded, width), f32),
            pltpu.VMEM((4, n_wide, 1, padded), f32),
            pltpu.VMEM((4 * n_wide, 1, padded), f32),
            dma((4,)),
            dma((groups,)),
            dma((2,)),
            dma((2,)),
            dma((n_wide,)),
            dma((n_wide,)),
            dma((4 * n_wide,)),
            dma((4 * n_wide,)),
        ],
        compiler_params=pltpu.CompilerParams(
            collective_id=0, has_side_effects=True, vmem_limit_bytes=60 * 1024 * 1024
        ),
    )(
        assignment,
        padding,
        activations.reshape(tokens, features),
        deltas.reshape(tokens, features),
        act_factor,
        delta_factor,
        queries.reshape(n_queries * rows, columns),
    )


def solution(mesh):
    placed = (
        P(("parts", "wide"), "sub", None),
        P(("parts", "wide"), "sub", None),
        P(None, "rep"),
        P(None, "rep"),
        P(None, ("rep", "wide"), "sub"),
        P("parts"),
        P(("parts", "wide")),
    )
    n_wide, n_rep, n_sub = (mesh.shape[name] for name in ("wide", "rep", "sub"))

    def shards(activations, deltas, act_factor, delta_factor, queries, assignment, padding):
        seq_dev, tokens, features = activations.shape
        n_queries, rows, columns = queries.shape
        fits = (
            seq_dev == 1
            and (n_rep, n_sub) == (2, 2)
            and n_wide <= 8
            and rows % 16 == 0
            and (n_wide * rows) % 128 == 0
            and columns % 128 == 0
            and act_factor.shape[1] == columns == n_wide * rows
            and tokens % 16 == 0
            and n_queries % (4 * GROUP) == 0
            and n_queries * rows * columns * 2 <= 44 * 2**20
        )
        run = functools.partial(fused_shards, n_wide) if fits else general_shards
        return run(activations, deltas, act_factor, delta_factor, queries, assignment, padding)

    return jax.shard_map(
        shards,
        mesh=mesh,
        in_specs=placed,
        out_specs=P(("parts", "wide"), ("rep", "sub")),
        check_vma=False,
    )
```

```python
import functools

import jax
import jax.numpy as jnp
from jax import lax
from jax.experimental import pallas as pl
from jax.experimental.pallas import tpu as pltpu
from jax.sharding import PartitionSpec as P

MESH = pl.DeviceIdType.MESH
GROUP = 160


def general_shards(
    activations, deltas, act_factor, delta_factor, queries, assignment, padding
):
    seq_dev, tok_dev, feature_width = activations.shape
    full_length = tok_dev * lax.axis_size("sub")
    token_start = lax.axis_index("sub") * tok_dev
    positions = token_start + lax.broadcasted_iota(jnp.int32, (seq_dev, tok_dev), 1)
    kept_mask = positions < (full_length - padding)[:, None]
    masked = jnp.where(kept_mask[:, :, None], deltas, jnp.zeros((), jnp.bfloat16))
    delta_proj = jnp.einsum(
        "stw,wi->sti", masked, delta_factor, preferred_element_type=jnp.float32
    ).astype(jnp.bfloat16)
    act_proj = jnp.einsum(
        "stw,wj->stj",
        activations,
        lax.all_gather(act_factor, "rep", axis=1, tiled=True),
        preferred_element_type=jnp.float32,
    ).astype(jnp.bfloat16)
    partial_value = jnp.einsum(
        "sti,stj->sij", delta_proj, act_proj, preferred_element_type=jnp.float32
    )
    summed = lax.psum_scatter(partial_value, "sub", scatter_dimension=2, tiled=True).astype(
        jnp.bfloat16
    )
    regrouped = lax.all_to_all(summed, "wide", split_axis=1, concat_axis=0, tiled=True)
    seq_total = regrouped.shape[0]
    grad_rows = regrouped.reshape(seq_total, -1)
    query_rows = queries.reshape(queries.shape[0], -1)
    partial_scores = lax.dot_general(
        grad_rows, query_rows, (((1,), (1,)), ((), ())), preferred_element_type=jnp.float32
    )
    inverse_order = (
        jnp.zeros((seq_total,), jnp.int32)
        .at[assignment]
        .set(jnp.arange(seq_total, dtype=jnp.int32))
    )
    ranked = jnp.take(partial_scores, inverse_order, axis=0)
    by_column = lax.psum_scatter(ranked, ("rep", "sub"), scatter_dimension=1, tiled=True)
    return lax.psum_scatter(by_column, "wide", scatter_dimension=0, tiled=True)


def kernel(
    n_wide,
    rows,
    assignment_ref,
    padding_ref,
    act_hbm,
    delta_hbm,
    act_factor_hbm,
    delta_factor_hbm,
    query_hbm,
    out_ref,
    act,
    delta,
    act_factor,
    delta_factor,
    query,
    diag,
    inner_mine,
    inner_theirs,
    factor_cols,
    grad,
    grad_all,
    weights,
    folded,
    outgoing,
    incoming,
    load_sem,
    query_sem,
    diag_sem,
    inner_sem,
    grad_send_sem,
    grad_recv_sem,
    score_send_sem,
    score_recv_sem,
):
    z = lax.axis_index("wide")
    r = lax.axis_index("rep")
    c = lax.axis_index("sub")
    n_rep, n_sub = 2, 2

    def peer(dz, dr, dc):
        return {
            "wide": lax.rem(z + dz, n_wide),
            "rep": lax.rem(r + dr, n_rep),
            "sub": lax.rem(c + dc, n_sub),
        }

    block_order = ((1, 1), (1, 0), (0, 1), (0, 0))
    everyone = [(0, 0, 1), (0, 1, 0)] + [(dz, 0, 0) for dz in range(n_wide - 1, 0, -1)]
    barrier = pltpu.get_barrier_semaphore()
    for offset in everyone:
        pl.semaphore_signal(barrier, inc=1, device_id=peer(*offset), device_id_type=MESH)

    loads = [
        pltpu.make_async_copy(src, dst, load_sem.at[k])
        for k, (src, dst) in enumerate(
            (
                (delta_factor_hbm, delta_factor),
                (delta_hbm, delta),
                (act_factor_hbm, act_factor),
                (act_hbm, act),
            )
        )
    ]
    for load in loads:
        load.start()

    chunk = GROUP * rows
    total = query.shape[0]
    block_groups = total // (chunk * n_rep * n_sub)

    def query_copy(place):
        span = pl.ds(pl.multiple_of(place * chunk, chunk), chunk)
        return pltpu.make_async_copy(query_hbm.at[span, :], query.at[span, :], query_sem.at[place])

    def block_at(dr, dc):
        return lax.rem(r + dr, n_rep) * n_sub + lax.rem(c + dc, n_sub)

    half = act_factor.shape[1]
    pl.semaphore_wait(barrier, len(everyone))
    diag_rows = pl.ds(pl.multiple_of(c * half, half), half)
    diag_copy = pltpu.make_async_remote_copy(
        src_ref=act_factor_hbm.at[diag_rows, :],
        dst_ref=diag,
        send_sem=diag_sem.at[0],
        recv_sem=diag_sem.at[1],
        device_id=peer(0, 1, 0),
        device_id_type=MESH,
    )

    @pl.when(r == c)
    def _():
        diag_copy.start()

    loads[0].wait()
    loads[1].wait()
    tokens = delta.shape[0]
    limit = n_sub * tokens - padding_ref[0] - c * tokens
    position = lax.broadcasted_iota(jnp.int32, (tokens, half), 0)
    projected = jnp.dot(delta[...], delta_factor[...], preferred_element_type=jnp.float32)
    delta_proj = jnp.where(position < limit, projected, 0.0).astype(jnp.bfloat16)

    loads[2].wait()
    loads[3].wait()
    for dr, dc in block_order:
        first = block_at(dr, dc) * block_groups

        def begin(t, carry, first=first):
            query_copy(first + t).start()
            return carry

        lax.fori_loop(0, block_groups, begin, 0)

    inner_mine[...] = lax.dot_general(
        delta_proj, act[...], (((0,), (0,)), ((), ())), preferred_element_type=jnp.float32
    )
    inner_copy = pltpu.make_async_remote_copy(
        src_ref=inner_mine,
        dst_ref=inner_theirs,
        send_sem=inner_sem.at[0],
        recv_sem=inner_sem.at[1],
        device_id=peer(0, 0, 1),
        device_id_type=MESH,
    )
    inner_copy.start()

    @pl.when(r == c)
    def _():
        factor_cols[...] = act_factor[...]
        diag_copy.wait_send()

    @pl.when(r != c)
    def _():
        mirrored = act_factor[diag_rows, :].astype(jnp.float32).T.astype(jnp.bfloat16)
        factor_cols[pl.ds(pl.multiple_of(r * half, half), half), :] = mirrored
        diag_copy.wait_recv()
        factor_cols[diag_rows, :] = diag[...]

    inner_copy.wait_recv()
    inner = inner_mine[...] + inner_theirs[...]
    high = inner.astype(jnp.bfloat16)
    low = (inner - high.astype(jnp.float32)).astype(jnp.bfloat16)
    gradient = jnp.dot(high, factor_cols[...], preferred_element_type=jnp.float32) + jnp.dot(
        low, factor_cols[...], preferred_element_type=jnp.float32
    )
    grad[...] = gradient.astype(jnp.bfloat16)
    mine = pl.ds(pl.multiple_of(z * rows, rows), rows)
    grad_copies = []
    for dz in range(n_wide - 1, 0, -1):
        target = pl.ds(pl.multiple_of(lax.rem(z + dz, n_wide) * rows, rows), rows)
        copy = pltpu.make_async_remote_copy(
            src_ref=grad.at[target, :],
            dst_ref=grad_all.at[mine, :],
            send_sem=grad_send_sem.at[dz],
            recv_sem=grad_recv_sem.at[dz],
            device_id=peer(dz, 0, 0),
            device_id_type=MESH,
        )
        copy.start()
        grad_copies.append(copy)
    grad_all[mine, :] = grad[mine, :]

    width = n_wide * rows
    lane = lax.broadcasted_iota(jnp.int32, (8, width), 1)
    sublane = lax.broadcasted_iota(jnp.int32, (8, width), 0)
    owner = lane // rows
    ranks = jnp.zeros((8, width), jnp.int32)
    for n in range(n_wide):
        ranks = jnp.where(owner == n, assignment_ref[n], ranks)
    places = jnp.where(ranks == sublane, 1.0, 0.0).astype(jnp.bfloat16)
    tile_of_lane = lax.rem(lane, rows) // 8
    on_diagonal = lax.rem(lane, 8) == sublane

    block_size = block_groups * GROUP
    folded[pl.ds(block_size, folded.shape[0] - block_size), :] = jnp.zeros(
        (folded.shape[0] - block_size, width), jnp.float32
    )
    inner_copy.wait_send()
    for copy in grad_copies:
        copy.wait_recv()
    weights[...] = grad_all[...].astype(jnp.float32).T.astype(jnp.bfloat16)

    def score_copy(k, dz):
        slot = k * n_wide + dz
        return pltpu.make_async_remote_copy(
            src_ref=outgoing.at[k, lax.rem(z + dz, n_wide)],
            dst_ref=incoming.at[slot],
            send_sem=score_send_sem.at[slot],
            recv_sem=score_recv_sem.at[slot],
            device_id=peer(dz, 1 - k // n_sub, 1 - lax.rem(k, n_sub)),
            device_id_type=MESH,
        )

    last = len(block_order) - 1

    def score_block(k, carry):
        first = block_at(1 - k // n_sub, 1 - lax.rem(k, n_sub)) * block_groups

        def score_group(t, inner_carry):
            query_copy(first + t).wait()
            span = pl.ds(pl.multiple_of((first + t) * chunk, chunk), chunk)
            products = jnp.dot(
                query[span, :], weights[...], preferred_element_type=jnp.float32
            ).reshape(GROUP, rows // 8, 8, width)
            chosen = products[:, 0]
            for a in range(1, rows // 8):
                chosen = jnp.where((tile_of_lane == a)[None], products[:, a], chosen)
            chosen = jnp.where(on_diagonal[None], chosen, 0.0)
            folded[pl.ds(pl.multiple_of(t * GROUP, GROUP), GROUP), :] = jnp.sum(chosen, axis=1)
            return inner_carry

        lax.fori_loop(0, block_groups, score_group, 0)
        sums = folded[...]
        sums_high = sums.astype(jnp.bfloat16)
        sums_low = (sums - sums_high.astype(jnp.float32)).astype(jnp.bfloat16)
        contract = (((1,), (1,)), ((), ()))
        ranked = lax.dot_general(
            places, sums_high, contract, preferred_element_type=jnp.float32
        ) + lax.dot_general(places, sums_low, contract, preferred_element_type=jnp.float32)
        for p in range(n_wide):
            outgoing[k, p] = ranked[p : p + 1, :]
        for dz in range(n_wide - 1, 0, -1):
            score_copy(k, dz).start()

        @pl.when(k < last)
        def _():
            score_copy(k, 0).start()

        return carry

    lax.fori_loop(0, len(block_order), score_block, 0)

    result = outgoing[last, z]
    for copy in grad_copies:
        copy.wait_send()
    for k in range(last + 1):
        for dz in range(n_wide - 1, -1, -1):
            if (k, dz) != (last, 0):
                score_copy(k, dz).wait()
                result = result + incoming[k * n_wide + dz]
    out_ref[...] = result[:, :block_size]


def fused_shards(
    n_wide, activations, deltas, act_factor, delta_factor, queries, assignment, padding
):
    _, tokens, features = activations.shape
    n_queries, rows, columns = queries.shape
    half = act_factor.shape[1]
    width = n_wide * rows
    groups = n_queries // GROUP
    block_size = n_queries // 4
    padded = -(-block_size // 128) * 128
    hbm = pl.BlockSpec(memory_space=pl.ANY)
    smem = pl.BlockSpec(memory_space=pltpu.SMEM)
    dma = pltpu.SemaphoreType.DMA
    bf16, f32 = jnp.bfloat16, jnp.float32
    return pl.pallas_call(
        functools.partial(kernel, n_wide, rows),
        out_shape=jax.ShapeDtypeStruct((1, block_size), f32),
        in_specs=[smem, smem] + [hbm] * 5,
        out_specs=pl.BlockSpec(memory_space=pltpu.VMEM),
        scratch_shapes=[
            pltpu.VMEM((tokens, features), bf16),
            pltpu.VMEM((tokens, features), bf16),
            pltpu.VMEM((features, half), bf16),
            pltpu.VMEM((features, half), bf16),
            pltpu.VMEM((n_queries * rows, columns), bf16),
            pltpu.VMEM((half, half), bf16),
            pltpu.VMEM((half, features), f32),
            pltpu.VMEM((half, features), f32),
            pltpu.VMEM((features, half), bf16),
            pltpu.VMEM((half, columns), bf16),
            pltpu.VMEM((width, columns), bf16),
            pltpu.VMEM((columns, width), bf16),
            pltpu.VMEM((padded, width), f32),
            pltpu.VMEM((4, n_wide, 1, padded), f32),
            pltpu.VMEM((4 * n_wide, 1, padded), f32),
            dma((4,)),
            dma((groups,)),
            dma((2,)),
            dma((2,)),
            dma((n_wide,)),
            dma((n_wide,)),
            dma((4 * n_wide,)),
            dma((4 * n_wide,)),
        ],
        compiler_params=pltpu.CompilerParams(
            collective_id=0, has_side_effects=True, vmem_limit_bytes=60 * 1024 * 1024
        ),
    )(
        assignment,
        padding,
        activations.reshape(tokens, features),
        deltas.reshape(tokens, features),
        act_factor,
        delta_factor,
        queries.reshape(n_queries * rows, columns),
    )


def solution(mesh):
    placed = (
        P(("parts", "wide"), "sub", None),
        P(("parts", "wide"), "sub", None),
        P(None, "rep"),
        P(None, "rep"),
        P(None, ("rep", "wide"), "sub"),
        P("parts"),
        P(("parts", "wide")),
    )
    n_wide, n_rep, n_sub = (mesh.shape[name] for name in ("wide", "rep", "sub"))

    def shards(activations, deltas, act_factor, delta_factor, queries, assignment, padding):
        seq_dev, tokens, features = activations.shape
        n_queries, rows, columns = queries.shape
        fits = (
            seq_dev == 1
            and (n_rep, n_sub) == (2, 2)
            and n_wide <= 8
            and rows % 16 == 0
            and (n_wide * rows) % 128 == 0
            and columns % 128 == 0
            and act_factor.shape[1] == columns == n_wide * rows
            and tokens % 16 == 0
            and n_queries % (4 * GROUP) == 0
            and n_queries * rows * columns * 2 <= 44 * 2**20
        )
        run = functools.partial(fused_shards, n_wide) if fits else general_shards
        return run(activations, deltas, act_factor, delta_factor, queries, assignment, padding)

    return jax.shard_map(
        shards,
        mesh=mesh,
        in_specs=placed,
        out_specs=P(("parts", "wide"), ("rep", "sub")),
        check_vma=False,
    )
```
